32 devices in a mesh: alpha: 4 (over z), beta: 8 (over y, x, core).
Axes of the slice: x: 2, y: 2, z: 4, core: 2. Of those that a mesh axis runs over, the one named last changes fastest.
Arguments:
- ci_vectors: float32 [4, 128, 1024], P(None, 'alpha', 'beta'), may hold values from -2 to 2
- alpha_source: int32 [128, 256], P('alpha'), may hold values from 0 to 127, as said below
- alpha_sign: int32 [128, 256], P('alpha'), may hold values from -1 to 1, as said below
- beta_source: int32 [1024, 256], P('beta'), may hold values from 0 to 1023, as said below
- beta_sign: int32 [1024, 256], P('beta'), may hold values from -1 to 1, as said below
Outputs:
- one_body: float32 [4, 1024], replicated
- two_body: float32 [1024, 1024], P(('alpha', 'beta'))
The draws below stay inside these ranges and needn't reach their ends.
Inputs may be any that keep to these rules, and one draw needn't show every extreme that they name: `alpha_source`: the source of a diagonal pair p p is the string itself. `beta_source`: the source of a diagonal pair p p is the string itself. `alpha_sign`: each string has 8 occupied orbitals; the sign is nonzero exactly where p is occupied and q equals p or is empty, 72 pairs a string, and is +1 on diagonal pairs. `beta_sign`: each string has 8 occupied orbitals; the sign is nonzero exactly where p is occupied and q equals p or is empty, 72 pairs a string, and is +1 on diagonal pairs.
All inputs are finite; a program needn't handle non-finite values.
Results may differ from the reference program's by a relative error of at most 0.0003.
Values sent between devices are 32-bit elements; how exact they have to be, the bound alone decides.
No kernel may reach another device: no remote copies, remote signals or barrier semaphores. Data moves between devices by JAX's collectives and lax.ppermute only.
A program may use at most 128 MiB of HBM per device.

```python
import jax
import jax.numpy as jnp
from jax import lax

NORB = 16
NELEC = 8
NSTATE = 4
B_DEV = 128
NA = 128
NB = 1024


def draw_ci_vectors(key, part):
    normal_part = jnp.clip(jax.random.normal(jax.random.fold_in(key, 11), (NSTATE, NA, NB), jnp.float32), -4.0, 4.0)
    alpha_scale = jax.random.uniform(jax.random.fold_in(key, 12), (NSTATE, NA, 1), jnp.float32, -2.0, 2.0)
    beta_scale = jax.random.uniform(jax.random.fold_in(key, 13), (NSTATE, 1, NB), jnp.float32, -2.0, 2.0)
    factor = 1.0 / jnp.sqrt(46.55 * NA * NB)
    return normal_part * jnp.exp(alpha_scale + beta_scale) * factor


def source_table(key, count):
    drawn = jax.random.randint(key, (count, NORB * NORB), 0, count, jnp.int32)
    pair_ids = jnp.arange(NORB * NORB, dtype=jnp.int32)
    diagonal = pair_ids // NORB == pair_ids % NORB
    own = jnp.arange(count, dtype=jnp.int32)[:, None]
    return jnp.where(diagonal[None, :], own, drawn)


def sign_table(key, count):
    scores = jax.random.randint(jax.random.fold_in(key, 21), (count, NORB), 0, 2 ** 20, jnp.int32)
    scores = scores * NORB + jnp.arange(NORB, dtype=jnp.int32)[None, :]
    ranks = jnp.argsort(jnp.argsort(scores, axis=1, stable=True), axis=1, stable=True)
    occupied = ranks < NELEC
    pair_ids = jnp.arange(NORB * NORB, dtype=jnp.int32)
    upper = pair_ids // NORB
    lower = pair_ids % NORB
    occ_upper = jnp.take(occupied, upper, axis=1)
    occ_lower = jnp.take(occupied, lower, axis=1)
    diagonal = (upper == lower)[None, :]
    valid = occ_upper & (diagonal | jnp.logical_not(occ_lower))
    flips = jax.random.randint(jax.random.fold_in(key, 22), (count, NORB * NORB), 0, 2, jnp.int32) * 2 - 1
    signs = jnp.where(diagonal, 1, flips)
    return jnp.where(valid, signs, 0).astype(jnp.int32)


def draw_alpha_source(key, part):
    return source_table(jax.random.fold_in(key, 31), NA)


def draw_alpha_sign(key, part):
    return sign_table(jax.random.fold_in(key, 32), NA)


def draw_beta_source(key, part):
    return source_table(jax.random.fold_in(key, 33), NB)


def draw_beta_sign(key, part):
    return sign_table(jax.random.fold_in(key, 34), NB)


def setup_inputs(seed: int = 0) -> dict:
    keys = jax.random.split(jax.random.key(seed), 6)
    ci_vectors = draw_ci_vectors(jax.random.fold_in(keys[5], 71), 0)
    alpha_source = draw_alpha_source(jax.random.fold_in(keys[5], 71), 0)
    alpha_sign = draw_alpha_sign(jax.random.fold_in(keys[5], 71), 0)
    beta_source = draw_beta_source(jax.random.fold_in(keys[5], 71), 0)
    beta_sign = draw_beta_sign(jax.random.fold_in(keys[5], 71), 0)
    return {"ci_vectors": ci_vectors, "alpha_source": alpha_source, "alpha_sign": alpha_sign, "beta_source": beta_source, "beta_sign": beta_sign}


def block_terms(ci_vectors, alpha_source, alpha_sign, beta_source, beta_sign, first_col):
    state_count = ci_vectors.shape[0]
    alpha_count = ci_vectors.shape[1]
    pair_count = alpha_source.shape[1]
    width = B_DEV
    local = lax.dynamic_slice_in_dim(ci_vectors, first_col, width, 2)
    alpha_part = jnp.take(local, alpha_source.T.reshape(-1), axis=1)
    alpha_part = alpha_part.reshape(state_count, pair_count, alpha_count, width)
    alpha_part = alpha_part * alpha_sign.T.astype(jnp.float32)[None, :, :, None]
    sources = lax.dynamic_slice_in_dim(beta_source, first_col, width, 0)
    signs = lax.dynamic_slice_in_dim(beta_sign, first_col, width, 0)
    beta_part = jnp.take(ci_vectors, sources.T.reshape(-1), axis=2)
    beta_part = beta_part.reshape(state_count, alpha_count, pair_count, width)
    beta_part = beta_part * signs.T.astype(jnp.float32)[None, None, :, :]
    excited = alpha_part + jnp.swapaxes(beta_part, 1, 2)
    excited_rows = excited.reshape(state_count * pair_count, alpha_count * width)
    one_term = lax.dot_general(local.reshape(state_count, alpha_count * width), excited_rows,
                               (((1,), (1,)), ((), ())), precision=lax.Precision.HIGHEST,
                               preferred_element_type=jnp.float32)
    rounded = excited_rows.astype(jnp.bfloat16)
    two_term = jnp.dot(rounded, rounded.T, preferred_element_type=jnp.float32)
    return one_term, two_term


def reference(ci_vectors, alpha_source, alpha_sign, beta_source, beta_sign):
    state_count = ci_vectors.shape[0]
    pair_count = alpha_source.shape[1]
    total = state_count * pair_count
    starts = jnp.arange(NB // B_DEV, dtype=jnp.int32) * B_DEV

    def step(carry, first_col):
        one_term, two_term = block_terms(ci_vectors, alpha_source, alpha_sign, beta_source, beta_sign, first_col)
        return (carry[0] + one_term, carry[1] + two_term), None

    start_carry = (jnp.zeros((state_count, total), jnp.float32), jnp.zeros((total, total), jnp.float32))
    final, unused = lax.scan(step, start_carry, starts)
    return final[0], final[1]
```

```python
import functools

import jax
import jax.numpy as jnp
import numpy as np
from jax import lax
from jax.experimental import pallas as pl
from jax.experimental.pallas import tpu as pltpu
from jax.sharding import PartitionSpec as P

F32 = jnp.float32
BF16 = jnp.bfloat16
LANES = 128


def pair_lanes(norb):
    forward, backward = [], []
    for p in range(norb):
        for q in range(p + 1, norb):
            forward.append(p * norb + q)
            backward.append(q * norb + p)
    for p in range(norb // 2):
        forward.append(p * (norb + 1))
        backward.append((p + norb // 2) * (norb + 1))
    return np.array(forward, np.int32), np.array(backward, np.int32)


def pick_lanes(left, right, lane):
    low = jnp.broadcast_to(lane & (LANES - 1), left.shape)
    from_left = jnp.take_along_axis(left, low, axis=1)
    from_right = jnp.take_along_axis(right, low, axis=1)
    return jnp.where(lane < LANES, from_left, from_right)


def split_two(value):
    high = value.astype(BF16)
    return high, (value - high.astype(F32)).astype(BF16)


def main_kernel(
    rows_each,
    orders,
    columns,
    place_ref,
    lane_ref,
    alpha_ref,
    beta_ref,
    flat_ref,
    asrc_ref,
    asgn_ref,
    bsrc_ref,
    bsgn_ref,
    *refs,
):
    streams = len(columns)
    send_refs = refs[:streams]
    keep_refs = refs[streams : 2 * streams]
    one_ref = refs[2 * streams]
    (
        table_ref,
        turned_ref,
        aidx_ref,
        asf_ref,
        asb_ref,
        bidx_ref,
        bsf_ref,
        bsb_ref,
        right_ref,
        low_ref,
        left_ref,
        state_ref,
        perm_ref,
    ) = refs[2 * streams + 1 :]
    states, alpha_count, beta_rows = alpha_ref.shape
    alpha_rows = beta_ref.shape[1]
    beta_count = beta_ref.shape[2]
    both = states * alpha_rows
    pairs = 2 * LANES
    my_alpha = place_ref[0]
    my_beta = place_ref[1]
    forward = lane_ref[0:1, 0:LANES]
    backward = lane_ref[0:1, LANES:pairs]

    def tables(src_ref, sgn_ref, idx_ref, sf_ref, sb_ref, count):
        for r in range(0, count, 8):
            rows = slice(r, r + 8)
            s0, s1 = sgn_ref[rows, 0:LANES], sgn_ref[rows, LANES:pairs]
            i0, i1 = src_ref[rows, 0:LANES], src_ref[rows, LANES:pairs]
            sf = pick_lanes(s0, s1, forward)
            sb = pick_lanes(s0, s1, backward)
            idx_ref[rows, :] = jnp.where(
                sf != 0, pick_lanes(i0, i1, forward), pick_lanes(i0, i1, backward)
            )
            sf_ref[rows, :] = sf.astype(F32)
            sb_ref[rows, :] = sb.astype(F32)

    tables(asrc_ref, asgn_ref, aidx_ref, asf_ref, asb_ref, alpha_rows)
    tables(bsrc_ref, bsgn_ref, bidx_ref, bsf_ref, bsb_ref, beta_rows)

    whole = beta_ref[...].reshape(both, beta_count)
    high, mid = split_two(whole)
    table_ref[0:both, :] = high
    table_ref[both : 2 * both, :] = mid
    for j in range(states):
        turned_ref[j] = alpha_ref[j].T

    flat = flat_ref[...]
    flat_high = flat.astype(BF16).astype(F32)
    flat_mid = flat - flat_high
    pad = jnp.zeros((16 - 2 * states, flat.shape[1]), F32)
    state_ref[...] = jnp.concatenate([flat_high, flat_mid, pad], axis=0).astype(BF16)

    natural = lane_ref[0:1, :]
    row = lax.broadcasted_iota(jnp.int32, (pairs, pairs), 0)
    shift = rows_each.bit_length() - 1
    wanted = (((row >> shift) ^ my_beta) << shift) | (row & (rows_each - 1))
    perm_ref[...] = jnp.where(natural == wanted, 1.0, 0.0).astype(BF16)

    chunk = min(1024, beta_count)
    chunks = beta_count // chunk
    step = 4

    def one_hot_dot(idx0, idx1, first):
        where = lax.broadcasted_iota(jnp.int32, (chunk, LANES), 0) + first
        picks = jnp.concatenate(
            [
                jnp.where(where == idx0, 1.0, 0.0).astype(BF16),
                jnp.where(where == idx1, 1.0, 0.0).astype(BF16),
            ],
            axis=1,
        )
        if chunks == 1:
            part = table_ref[...]
        else:
            part = table_ref[:, pl.ds(pl.multiple_of(first, chunk), chunk)]
        return jnp.dot(part, picks, preferred_element_type=F32)

    def build(block, carry):
        for u in range(step // 2):
            b0 = block * step + 2 * u
            idx0 = bidx_ref[pl.ds(b0, 1), :]
            idx1 = bidx_ref[pl.ds(b0 + 1, 1), :]
            if chunks == 1:
                got = one_hot_dot(idx0, idx1, 0)
            else:
                got = lax.fori_loop(
                    0,
                    chunks,
                    lambda c, acc: acc + one_hot_dot(idx0, idx1, c * chunk),
                    jnp.zeros((2 * both, 2 * LANES), F32),
                )
            picked = got[0:both] + got[both : 2 * both]
            for v in range(2):
                b = b0 + v
                sf = bsf_ref[pl.ds(b, 1), :]
                sb = bsb_ref[pl.ds(b, 1), :]
                first = pl.multiple_of(b * alpha_rows, alpha_rows)
                for j in range(states):
                    source = jnp.broadcast_to(turned_ref[j, pl.ds(b, 1), :], (8, LANES))
                    from_alpha = jnp.concatenate(
                        [
                            jnp.take_along_axis(source, aidx_ref[r : r + 8, :], axis=1)
                            for r in range(0, alpha_rows, 8)
                        ],
                        axis=0,
                    )
                    from_beta = picked[
                        j * alpha_rows : (j + 1) * alpha_rows, v * LANES : (v + 1) * LANES
                    ]
                    for half, asg, bsg in ((0, asf_ref, sf), (1, asb_ref, sb)):
                        value = asg[...] * from_alpha + bsg * from_beta
                        top, rest = split_two(value)
                        col = j * pairs + half * LANES
                        right_ref[pl.ds(first, alpha_rows), col : col + LANES] = top
                        low_ref[pl.ds(first, alpha_rows), col : col + LANES] = rest
        return carry

    lax.fori_loop(0, beta_rows // step, build, 0)

    depth = alpha_rows * beta_rows
    piece = 512

    def turn(k, carry):
        first = pl.multiple_of(k * piece, piece)
        for ja in range(states):
            col = pl.multiple_of((my_alpha ^ ja) * pairs, pairs)
            value = lax.dot_general(
                perm_ref[...],
                right_ref[pl.ds(first, piece), pl.ds(col, pairs)],
                (((1,), (1,)), ((), ())),
                preferred_element_type=F32,
            )
            left_ref[ja * pairs : (ja + 1) * pairs, pl.ds(first, piece)] = value.astype(BF16)
        return carry

    lax.fori_loop(0, depth // piece, turn, 0)

    beta_bits = (pairs // rows_each).bit_length() - 1
    for ja in range(states):
        value = jnp.dot(
            left_ref[ja * pairs : (ja + 1) * pairs, :],
            right_ref[...],
            preferred_element_type=F32,
        )
        for jb in range(1 << beta_bits):
            rows = value[jb * rows_each : (jb + 1) * rows_each]
            first_col = 0
            for s in range(streams):
                place = 0
                for kind, bit in orders[s]:
                    source = jb if kind == "beta" else ja
                    place = 2 * place + ((source >> bit) & 1)
                target = send_refs[s] if jb & 1 else keep_refs[s]
                target[place * rows_each : (place + 1) * rows_each, :] = rows[
                    :, first_col : first_col + columns[s]
                ]
                first_col += columns[s]

    one = jnp.dot(state_ref[...], right_ref[...], preferred_element_type=F32)
    one_low = jnp.dot(state_ref[...], low_ref[...], preferred_element_type=F32)
    total = one + one_low
    one_ref[...] = total[0:states] + total[states : 2 * states]


def last_kernel(columns, lane_ref, one_a_ref, one_b_ref, *refs):
    streams = len(columns)
    kept, got = refs[:streams], refs[streams : 2 * streams]
    one_ref, two_ref = refs[2 * streams :]
    pairs = 2 * LANES
    back0, back1 = lane_ref[0:1, 0:LANES], lane_ref[0:1, LANES:pairs]
    value = jnp.concatenate([kept[s][...] + got[s][...] for s in range(streams)], axis=1)

    def place(whole, out_ref):
        rows, total = whole.shape
        for col in range(0, total, pairs):
            for r in range(0, rows, 8):
                n = min(8, rows - r)
                left = whole[r : r + n, col : col + LANES]
                right = whole[r : r + n, col + LANES : col + pairs]
                out_ref[r : r + n, col : col + LANES] = pick_lanes(left, right, back0)
                out_ref[r : r + n, col + LANES : col + pairs] = pick_lanes(left, right, back1)

    def full(whole):
        rows = whole.shape[0]
        if rows % 8 == 0:
            return whole
        return jnp.concatenate([whole] * (8 // rows), axis=0)

    place_rows(place, full, value, two_ref)
    place_rows(place, full, one_a_ref[...] + one_b_ref[...], one_ref)


def place_rows(place, full, whole, out_ref):
    rows = whole.shape[0]
    if rows % 8 == 0:
        place(whole, out_ref)
        return

    class Cut:
        def __setitem__(self, where, value):
            out_ref[0:rows, where[1]] = value[0:rows]

    place(full(whole), Cut())


def swap(value, kind, bit, size):
    return lax.ppermute(value, kind, [(i, i ^ (1 << bit)) for i in range(size)])


def shards(sizes, ci_vectors, alpha_source, alpha_sign, beta_source, beta_sign):
    states, alpha_rows, beta_rows = ci_vectors.shape
    pairs = alpha_source.shape[1]
    total = states * pairs
    norb = int(round(pairs ** 0.5))
    forward, backward = pair_lanes(norb)
    lane = np.concatenate([forward, backward]).reshape(1, pairs)
    inverse = np.argsort(lane[0]).astype(np.int32).reshape(1, pairs)
    rows_each = total // (sizes["alpha"] * sizes["beta"])
    alpha_bits = sizes["alpha"].bit_length() - 1
    beta_bits = sizes["beta"].bit_length() - 1

    alpha_whole = lax.all_gather(ci_vectors, "alpha", axis=1, tiled=True)
    beta_whole = lax.all_gather(ci_vectors, "beta", axis=2, tiled=True)
    flat = jnp.transpose(ci_vectors, (0, 2, 1)).reshape(states, alpha_rows * beta_rows)
    place = jnp.stack([lax.axis_index("alpha"), lax.axis_index("beta")]).astype(jnp.int32)

    in_beta = [("beta", i) for i in range(1, beta_bits)]
    in_alpha = [("alpha", i) for i in range(alpha_bits)]
    orders = [
        in_beta + in_alpha,
        in_beta[1:] + in_alpha + in_beta[:1],
        in_alpha + in_beta,
    ]
    columns = [384, 384, 256]
    streams = len(orders)
    half = total // 2
    beta_count = beta_whole.shape[2]
    depth = alpha_rows * beta_rows
    vmem = pl.BlockSpec(memory_space=pltpu.VMEM)
    results = pl.pallas_call(
        functools.partial(main_kernel, rows_each, orders, columns),
        out_shape=[jax.ShapeDtypeStruct((half, c), F32) for c in columns] * 2
        + [jax.ShapeDtypeStruct((states, total), F32)],
        in_specs=[pl.BlockSpec(memory_space=pltpu.SMEM)] + [vmem] * 8,
        out_specs=[vmem] * (2 * streams + 1),
        scratch_shapes=[
            pltpu.VMEM((2 * states * alpha_rows, beta_count), BF16),
            pltpu.VMEM((states, beta_rows, alpha_whole.shape[1]), F32),
            pltpu.VMEM((alpha_rows, LANES), jnp.int32),
            pltpu.VMEM((alpha_rows, LANES), F32),
            pltpu.VMEM((alpha_rows, LANES), F32),
            pltpu.VMEM((beta_rows, LANES), jnp.int32),
            pltpu.VMEM((beta_rows, LANES), F32),
            pltpu.VMEM((beta_rows, LANES), F32),
            pltpu.VMEM((depth, total), BF16),
            pltpu.VMEM((depth, total), BF16),
            pltpu.VMEM((total, depth), BF16),
            pltpu.VMEM((16, depth), BF16),
            pltpu.VMEM((pairs, pairs), BF16),
        ],
        compiler_params=pltpu.CompilerParams(vmem_limit_bytes=58 << 20),
        name="excite",
    )(
        place,
        jnp.asarray(lane),
        alpha_whole,
        beta_whole,
        flat,
        alpha_source,
        alpha_sign,
        beta_source,
        beta_sign,
    )
    send, keep, one = list(results[:streams]), list(results[streams:-1]), results[-1]
    got = [swap(send[s], "beta", 0, sizes["beta"]) for s in range(streams)]
    one = one + swap(one, "beta", 0, sizes["beta"])
    steps = len(orders[0])
    for t in range(steps):
        for s in range(streams):
            kind, bit = orders[s][t]
            n = keep[s].shape[0] // 2
            out = keep[s][n:] + got[s][n:]
            mine = keep[s][:n] + got[s][:n]
            got[s] = swap(out, kind, bit, sizes[kind])
            keep[s] = mine
        kind, bit = orders[0][t]
        if t < steps - 1:
            one = one + swap(one, kind, bit, sizes[kind])
        else:
            other = swap(one, kind, bit, sizes[kind])
    one_body, two_body = pl.pallas_call(
        functools.partial(last_kernel, columns),
        out_shape=[
            jax.ShapeDtypeStruct((states, total), F32),
            jax.ShapeDtypeStruct((rows_each, total), F32),
        ],
        in_specs=[vmem] * (3 + 2 * streams),
        out_specs=[vmem] * 2,
        name="finish",
    )(jnp.asarray(inverse), one, other, *keep, *got)
    return (one_body, two_body)


def solution(mesh):
    return jax.shard_map(
        functools.partial(shards, dict(mesh.shape)),
        mesh=mesh,
        in_specs=(
            P(None, "alpha", "beta"),
            P("alpha", None),
            P("alpha", None),
            P("beta", None),
            P("beta", None),
        ),
        out_specs=(P(), P(("alpha", "beta"), None)),
        check_vma=False,
    )
```

```python
import functools

import jax
import jax.numpy as jnp
import numpy as np
from jax import lax
from jax.experimental import pallas as pl
from jax.experimental.pallas import tpu as pltpu
from jax.sharding import PartitionSpec as P

F32 = jnp.float32
BF16 = jnp.bfloat16
LANES = 128
ONE_ROWS = 16


def pair_lanes(norb):
    forward, backward = [], []
    for p in range(norb):
        for q in range(p + 1, norb):
            forward.append(p * norb + q)
            backward.append(q * norb + p)
    for p in range(norb // 2):
        forward.append(p * (norb + 1))
        backward.append((p + norb // 2) * (norb + 1))
    return np.array(forward, np.int32), np.array(backward, np.int32)


def pick_lanes(left, right, lane):
    low = jnp.broadcast_to(lane & (LANES - 1), left.shape)
    from_left = jnp.take_along_axis(left, low, axis=1)
    from_right = jnp.take_along_axis(right, low, axis=1)
    return jnp.where(lane < LANES, from_left, from_right)


def split_two(value):
    high = value.astype(BF16)
    return high, (value - high.astype(F32)).astype(BF16)


def main_kernel(
    rows_each,
    orders,
    columns,
    parts,
    place_ref,
    lane_ref,
    flat_ref,
    asrc_ref,
    asgn_ref,
    bsrc_ref,
    bsgn_ref,
    *refs,
):
    alpha_parts, beta_parts = parts
    alpha_refs = refs[:alpha_parts]
    beta_refs = (refs[0],) + refs[alpha_parts : alpha_parts + beta_parts - 1]
    refs = refs[alpha_parts + beta_parts - 1 :]
    streams = len(columns)
    send_refs = refs[:streams]
    keep_refs = refs[streams : 2 * streams]
    (
        table_ref,
        turned_ref,
        aidx_ref,
        asf_ref,
        asb_ref,
        bidx_ref,
        bsf_ref,
        bsb_ref,
        right_ref,
        low_ref,
        left_ref,
        state_ref,
        perm_ref,
    ) = refs[2 * streams :]
    states, alpha_rows, beta_rows = alpha_refs[0].shape
    beta_count = beta_parts * beta_rows
    both = states * alpha_rows
    pairs = 2 * LANES
    my_alpha = place_ref[0]
    my_beta = place_ref[1]
    forward = lane_ref[0:1, 0:LANES]
    backward = lane_ref[0:1, LANES:pairs]

    def tables(src_ref, sgn_ref, idx_ref, sf_ref, sb_ref, count, flip):
        for r in range(0, count, 8):
            rows = slice(r, r + 8)
            s0, s1 = sgn_ref[rows, 0:LANES], sgn_ref[rows, LANES:pairs]
            i0, i1 = src_ref[rows, 0:LANES], src_ref[rows, LANES:pairs]
            sf = pick_lanes(s0, s1, forward)
            sb = pick_lanes(s0, s1, backward)
            source = jnp.where(
                sf != 0, pick_lanes(i0, i1, forward), pick_lanes(i0, i1, backward)
            )
            idx_ref[rows, :] = source ^ flip
            sf_ref[rows, :] = sf.astype(F32)
            sb_ref[rows, :] = sb.astype(F32)

    tables(asrc_ref, asgn_ref, aidx_ref, asf_ref, asb_ref, alpha_rows, my_alpha * alpha_rows)
    tables(bsrc_ref, bsgn_ref, bidx_ref, bsf_ref, bsb_ref, beta_rows, my_beta * beta_rows)

    for k in range(beta_parts):
        high, mid = split_two(beta_refs[k][...].reshape(both, beta_rows))
        table_ref[0:both, k * beta_rows : (k + 1) * beta_rows] = high
        table_ref[both : 2 * both, k * beta_rows : (k + 1) * beta_rows] = mid
    for j in range(states):
        rows = jnp.concatenate([alpha_refs[k][j] for k in range(alpha_parts)], axis=0)
        turned_ref[j] = rows.T

    flat = flat_ref[...]
    flat_high = flat.astype(BF16).astype(F32)
    flat_mid = flat - flat_high
    pad = jnp.zeros((16 - 2 * states, flat.shape[1]), F32)
    state_ref[...] = jnp.concatenate([flat_high, flat_mid, pad], axis=0).astype(BF16)

    natural = lane_ref[0:1, :]
    row = lax.broadcasted_iota(jnp.int32, (pairs, pairs), 0)
    shift = rows_each.bit_length() - 1
    wanted = (((row >> shift) ^ my_beta) << shift) | (row & (rows_each - 1))
    perm_ref[...] = jnp.where(natural == wanted, 1.0, 0.0).astype(BF16)

    chunk = min(1024, beta_count)
    chunks = beta_count // chunk
    step = 16

    def one_hot_dot(idx0, idx1, first):
        where = lax.broadcasted_iota(jnp.int32, (chunk, LANES), 0) + first
        picks = jnp.concatenate(
            [
                jnp.where(where == idx0, 1.0, 0.0).astype(BF16),
                jnp.where(where == idx1, 1.0, 0.0).astype(BF16),
            ],
            axis=1,
        )
        if chunks == 1:
            part = table_ref[...]
        else:
            part = table_ref[:, pl.ds(pl.multiple_of(first, chunk), chunk)]
        return jnp.dot(part, picks, preferred_element_type=F32)

    def build(block, carry):
        for u in range(step // 2):
            b0 = block * step + 2 * u
            idx0 = bidx_ref[pl.ds(b0, 1), :]
            idx1 = bidx_ref[pl.ds(b0 + 1, 1), :]
            if chunks == 1:
                got = one_hot_dot(idx0, idx1, 0)
            else:
                got = lax.fori_loop(
                    0,
                    chunks,
                    lambda c, acc: acc + one_hot_dot(idx0, idx1, c * chunk),
                    jnp.zeros((2 * both, 2 * LANES), F32),
                )
            picked = got[0:both] + got[both : 2 * both]
            for v in range(2):
                b = b0 + v
                sf = bsf_ref[pl.ds(b, 1), :]
                sb = bsb_ref[pl.ds(b, 1), :]
                first = pl.multiple_of(b * alpha_rows, alpha_rows)
                for j in range(states):
                    source = jnp.broadcast_to(turned_ref[j, pl.ds(b, 1), :], (8, LANES))
                    from_alpha = jnp.concatenate(
                        [
                            jnp.take_along_axis(source, aidx_ref[r : r + 8, :], axis=1)
                            for r in range(0, alpha_rows, 8)
                        ],
                        axis=0,
                    )
                    from_beta = picked[
                        j * alpha_rows : (j + 1) * alpha_rows, v * LANES : (v + 1) * LANES
                    ]
                    for half, asg, bsg in ((0, asf_ref, sf), (1, asb_ref, sb)):
                        value = asg[...] * from_alpha + bsg * from_beta
                        top, rest = split_two(value)
                        col = j * pairs + half * LANES
                        right_ref[pl.ds(first, alpha_rows), col : col + LANES] = top
                        low_ref[pl.ds(first, alpha_rows), col : col + LANES] = rest
        return carry

    lax.fori_loop(0, beta_rows // step, build, 0)

    depth = alpha_rows * beta_rows
    piece = 512

    def turn(k, carry):
        first = pl.multiple_of(k * piece, piece)
        for ja in range(states):
            col = pl.multiple_of((my_alpha ^ ja) * pairs, pairs)
            value = lax.dot_general(
                perm_ref[...],
                right_ref[pl.ds(first, piece), pl.ds(col, pairs)],
                (((1,), (1,)), ((), ())),
                preferred_element_type=F32,
            )
            left_ref[ja * pairs : (ja + 1) * pairs, pl.ds(first, piece)] = value.astype(BF16)
        return carry

    lax.fori_loop(0, depth // piece, turn, 0)

    beta_bits = (pairs // rows_each).bit_length() - 1
    for ja in range(states):
        value = jnp.dot(
            left_ref[ja * pairs : (ja + 1) * pairs, :],
            right_ref[...],
            preferred_element_type=F32,
        )
        for jb in range(1 << beta_bits):
            rows = value[jb * rows_each : (jb + 1) * rows_each]
            first_col = 0
            for s in range(streams):
                place = 0
                for kind, bit in orders[s]:
                    source = jb if kind == "beta" else ja
                    place = 2 * place + ((source >> bit) & 1)
                target = send_refs[s] if jb & 1 else keep_refs[s]
                first_row = place * rows_each + (ONE_ROWS if s == streams - 1 else 0)
                target[first_row : first_row + rows_each, :] = rows[
                    :, first_col : first_col + columns[s]
                ]
                first_col += columns[s]

    one = jnp.dot(state_ref[...], right_ref[...], preferred_element_type=F32)
    one_low = jnp.dot(state_ref[...], low_ref[...], preferred_element_type=F32)
    total = one + one_low
    one = total[0:states] + total[states : 2 * states]
    one_rows = jnp.concatenate(
        [one[:, j * pairs : (j + 1) * pairs] for j in range(states)], axis=0
    )
    send_refs[-1][0:ONE_ROWS, :] = one_rows
    keep_refs[-1][0:ONE_ROWS, :] = one_rows


def last_kernel(groups, lane_ref, *refs):
    count = len(groups)
    kept, got = refs[:count], refs[count : 2 * count]
    one_ref, two_ref = refs[2 * count :]
    pairs = 2 * LANES
    back0, back1 = lane_ref[0:1, 0:LANES], lane_ref[0:1, LANES:pairs]
    sums = [kept[s][...] + got[s][...] for s in range(count)]
    one_rows = sums[-1][0:ONE_ROWS]
    states = ONE_ROWS // one_ref.shape[0]
    sums[-1] = sums[-1][ONE_ROWS:]
    value = jnp.concatenate(sums, axis=1)

    def place(whole, out_ref, first_col):
        rows, total = whole.shape
        for col in range(0, total, pairs):
            for r in range(0, rows, 8):
                n = min(8, rows - r)
                left = whole[r : r + n, col : col + LANES]
                right = whole[r : r + n, col + LANES : col + pairs]
                if n < 8:
                    left = jnp.concatenate([left] * (8 // n), axis=0)
                    right = jnp.concatenate([right] * (8 // n), axis=0)
                to = first_col + col
                out_ref[r : r + n, to : to + LANES] = pick_lanes(left, right, back0)[0:n]
                out_ref[r : r + n, to + LANES : to + pairs] = pick_lanes(left, right, back1)[0:n]

    place(value, two_ref, 0)
    rows = one_ref.shape[0]
    for j in range(states):
        place(one_rows[j * rows : (j + 1) * rows], one_ref, j * pairs)


def swap(value, kind, flip, sizes):
    return lax.ppermute(value, kind, [(i, i ^ flip) for i in range(sizes[kind])])


def shards(sizes, ci_vectors, alpha_source, alpha_sign, beta_source, beta_sign):
    states, alpha_rows, beta_rows = ci_vectors.shape
    pairs = alpha_source.shape[1]
    total = states * pairs
    norb = int(round(pairs ** 0.5))
    forward, backward = pair_lanes(norb)
    lane = np.concatenate([forward, backward]).reshape(1, pairs)
    inverse = np.argsort(lane[0]).astype(np.int32).reshape(1, pairs)
    rows_each = total // (sizes["alpha"] * sizes["beta"])
    alpha_bits = sizes["alpha"].bit_length() - 1
    beta_bits = sizes["beta"].bit_length() - 1

    beta_parts = [ci_vectors] + [None] * (sizes["beta"] - 1)
    alpha_parts = [ci_vectors] + [None] * (sizes["alpha"] - 1)
    beta_parts[1] = swap(ci_vectors, "beta", 1, sizes)
    for j in range(2, sizes["beta"], 2):
        beta_parts[j] = swap(ci_vectors, "beta", j, sizes)
    for j in range(1, sizes["alpha"]):
        alpha_parts[j] = swap(ci_vectors, "alpha", j, sizes)
    for j in range(2, sizes["beta"], 2):
        beta_parts[j + 1] = swap(beta_parts[j], "beta", 1, sizes)
    flat = jnp.transpose(ci_vectors, (0, 2, 1)).reshape(states, alpha_rows * beta_rows)
    place = jnp.stack([lax.axis_index("alpha"), lax.axis_index("beta")]).astype(jnp.int32)

    in_beta = [("beta", i) for i in range(1, beta_bits)]
    in_alpha = [("alpha", i) for i in range(alpha_bits)]
    orders = [
        in_beta + in_alpha,
        in_beta[::-1] + in_alpha,
        in_alpha + in_beta,
    ]
    columns = [384, 384, 256]
    streams = len(orders)
    extra = [0, 0, ONE_ROWS]
    half = total // 2
    beta_count = sizes["beta"] * beta_rows
    depth = alpha_rows * beta_rows
    vmem = pl.BlockSpec(memory_space=pltpu.VMEM)
    results = pl.pallas_call(
        functools.partial(
            main_kernel, rows_each, orders, columns, (sizes["alpha"], sizes["beta"])
        ),
        out_shape=[
            jax.ShapeDtypeStruct((half + extra[s], columns[s]), F32) for s in range(streams)
        ]
        * 2,
        in_specs=[pl.BlockSpec(memory_space=pltpu.SMEM)]
        + [vmem] * (5 + sizes["alpha"] + sizes["beta"]),
        out_specs=[vmem] * (2 * streams),
        scratch_shapes=[
            pltpu.VMEM((2 * states * alpha_rows, beta_count), BF16),
            pltpu.VMEM((states, beta_rows, sizes["alpha"] * alpha_rows), F32),
            pltpu.VMEM((alpha_rows, LANES), jnp.int32),
            pltpu.VMEM((alpha_rows, LANES), F32),
            pltpu.VMEM((alpha_rows, LANES), F32),
            pltpu.VMEM((beta_rows, LANES), jnp.int32),
            pltpu.VMEM((beta_rows, LANES), F32),
            pltpu.VMEM((beta_rows, LANES), F32),
            pltpu.VMEM((depth, total), BF16),
            pltpu.VMEM((depth, total), BF16),
            pltpu.VMEM((total, depth), BF16),
            pltpu.VMEM((16, depth), BF16),
            pltpu.VMEM((pairs, pairs), BF16),
        ],
        compiler_params=pltpu.CompilerParams(vmem_limit_bytes=58 << 20),
        name="excite",
    )(
        place,
        jnp.asarray(lane),
        flat,
        alpha_source,
        alpha_sign,
        beta_source,
        beta_sign,
        *alpha_parts,
        *beta_parts[1:],
    )
    send, keep = list(results[:streams]), list(results[streams:])
    got = [swap(send[s], "beta", 1, sizes) for s in range(streams)]
    for t in range(len(orders[0])):
        if t:
            keep, got = lax.optimization_barrier((keep, got))
        if len(keep) == 3 and orders[0][t:] == orders[1][t:]:
            keep = [jnp.concatenate(keep[:2], axis=1), keep[2]]
            got = [jnp.concatenate(got[:2], axis=1), got[2]]
            orders = orders[1:]
            extra = extra[1:]
        out = [None] * len(keep)
        for s in range(len(keep)):
            n = (keep[s].shape[0] - extra[s]) // 2 + extra[s]
            out[s] = keep[s][n:] + got[s][n:]
            if extra[s]:
                out[s] = jnp.concatenate([keep[s][: extra[s]] + got[s][: extra[s]], out[s]], axis=0)
            keep[s] = keep[s][:n] + got[s][:n]
        for s in range(len(keep)):
            kind, bit = orders[s][t]
            got[s] = swap(out[s], kind, 1 << bit, sizes)
    one_body, two_body = pl.pallas_call(
        functools.partial(last_kernel, [k.shape[1] for k in keep]),
        out_shape=[
            jax.ShapeDtypeStruct((states, total), F32),
            jax.ShapeDtypeStruct((rows_each, total), F32),
        ],
        in_specs=[vmem] * (1 + 2 * len(keep)),
        out_specs=[vmem] * 2,
        name="finish",
    )(jnp.asarray(inverse), *keep, *got)
    return (one_body, two_body)


def solution(mesh):
    return jax.shard_map(
        functools.partial(shards, dict(mesh.shape)),
        mesh=mesh,
        in_specs=(
            P(None, "alpha", "beta"),
            P("alpha", None),
            P("alpha", None),
            P("beta", None),
            P("beta", None),
        ),
        out_specs=(P(), P(("alpha", "beta"), None)),
        check_vma=False,
    )
```

```python
import functools

import jax
import jax.numpy as jnp
import numpy as np
from jax import lax
from jax.experimental import pallas as pl
from jax.experimental.pallas import tpu as pltpu
from jax.sharding import PartitionSpec as P

F32 = jnp.float32
BF16 = jnp.bfloat16
LANES = 128
ONE_ROWS = 16


def pair_lanes(norb):
    forward, backward = [], []
    for p in range(norb):
        for q in range(p + 1, norb):
            forward.append(p * norb + q)
            backward.append(q * norb + p)
    for p in range(norb // 2):
        forward.append(p * (norb + 1))
        backward.append((p + norb // 2) * (norb + 1))
    return np.array(forward, np.int32), np.array(backward, np.int32)


def pick_lanes(left, right, lane):
    low = jnp.broadcast_to(lane & (LANES - 1), left.shape)
    from_left = jnp.take_along_axis(left, low, axis=1)
    from_right = jnp.take_along_axis(right, low, axis=1)
    return jnp.where(lane < LANES, from_left, from_right)


def split_two(value):
    high = value.astype(BF16)
    return high, (value - high.astype(F32)).astype(BF16)


def main_kernel(
    rows_each,
    orders,
    columns,
    parts,
    lane_ref,
    flat_ref,
    asrc_ref,
    asgn_ref,
    bsrc_ref,
    bsgn_ref,
    *refs,
):
    alpha_parts, beta_parts = parts
    count = alpha_parts + beta_parts - 1
    given, refs = refs[:count], refs[count:]
    parts_ref, sems = refs[-2:]
    copies = [
        pltpu.make_async_copy(given[k], parts_ref.at[k], sems.at[k]) for k in range(count)
    ]
    for copy in copies:
        copy.start()
    streams = len(columns)
    send_refs = refs[:streams]
    keep_refs = refs[streams : 2 * streams]
    (
        table_ref,
        turned_ref,
        aidx_ref,
        asf_ref,
        asb_ref,
        bidx_ref,
        bsf_ref,
        bsb_ref,
        right_ref,
        low_ref,
        left_ref,
        state_ref,
        perm_ref,
    ) = refs[2 * streams : -2]
    states, alpha_rows, beta_rows = given[0].shape
    beta_count = beta_parts * beta_rows
    both = states * alpha_rows
    pairs = 2 * LANES
    my_alpha = lax.axis_index("alpha")
    my_beta = lax.axis_index("beta")
    forward = lane_ref[0:1, 0:LANES]
    backward = lane_ref[0:1, LANES:pairs]

    def tables(src_ref, sgn_ref, idx_ref, sf_ref, sb_ref, count, flip):
        for r in range(0, count, 8):
            rows = slice(r, r + 8)
            s0, s1 = sgn_ref[rows, 0:LANES], sgn_ref[rows, LANES:pairs]
            i0, i1 = src_ref[rows, 0:LANES], src_ref[rows, LANES:pairs]
            sf = pick_lanes(s0, s1, forward)
            sb = pick_lanes(s0, s1, backward)
            source = jnp.where(
                sf != 0, pick_lanes(i0, i1, forward), pick_lanes(i0, i1, backward)
            )
            idx_ref[rows, :] = source ^ flip
            sf_ref[rows, :] = sf.astype(F32)
            sb_ref[rows, :] = sb.astype(F32)

    tables(asrc_ref, asgn_ref, aidx_ref, asf_ref, asb_ref, alpha_rows, my_alpha * alpha_rows)
    tables(bsrc_ref, bsgn_ref, bidx_ref, bsf_ref, bsb_ref, beta_rows, my_beta * beta_rows)

    flat = flat_ref[...]
    flat_high = flat.astype(BF16).astype(F32)
    flat_mid = flat - flat_high
    pad = jnp.zeros((16 - 2 * states, flat.shape[1]), F32)
    state_ref[...] = jnp.concatenate([flat_high, flat_mid, pad], axis=0).astype(BF16)

    natural = lane_ref[0:1, :]
    row = lax.broadcasted_iota(jnp.int32, (pairs, pairs), 0)
    shift = rows_each.bit_length() - 1
    wanted = (((row >> shift) ^ my_beta) << shift) | (row & (rows_each - 1))
    perm_ref[...] = jnp.where(natural == wanted, 1.0, 0.0).astype(BF16)

    for copy in copies:
        copy.wait()
    for k in range(beta_parts):
        at = alpha_parts + k - 1 if k else 0
        high, mid = split_two(parts_ref[at].reshape(both, beta_rows))
        table_ref[0:both, k * beta_rows : (k + 1) * beta_rows] = high
        table_ref[both : 2 * both, k * beta_rows : (k + 1) * beta_rows] = mid
    for j in range(states):
        rows = jnp.concatenate([parts_ref[k, j] for k in range(alpha_parts)], axis=0)
        turned_ref[j] = rows.T

    chunk = min(1024, beta_count)
    chunks = beta_count // chunk
    step = 16

    def one_hot_dot(idx0, idx1, first):
        where = lax.broadcasted_iota(jnp.int32, (chunk, LANES), 0) + first
        picks = jnp.concatenate(
            [
                jnp.where(where == idx0, 1.0, 0.0).astype(BF16),
                jnp.where(where == idx1, 1.0, 0.0).astype(BF16),
            ],
            axis=1,
        )
        if chunks == 1:
            part = table_ref[...]
        else:
            part = table_ref[:, pl.ds(pl.multiple_of(first, chunk), chunk)]
        return jnp.dot(part, picks, preferred_element_type=F32)

    def build(block, carry):
        for u in range(step // 2):
            b0 = block * step + 2 * u
            idx0 = bidx_ref[pl.ds(b0, 1), :]
            idx1 = bidx_ref[pl.ds(b0 + 1, 1), :]
            if chunks == 1:
                got = one_hot_dot(idx0, idx1, 0)
            else:
                got = lax.fori_loop(
                    0,
                    chunks,
                    lambda c, acc: acc + one_hot_dot(idx0, idx1, c * chunk),
                    jnp.zeros((2 * both, 2 * LANES), F32),
                )
            picked = got[0:both] + got[both : 2 * both]
            for v in range(2):
                b = b0 + v
                sf = bsf_ref[pl.ds(b, 1), :]
                sb = bsb_ref[pl.ds(b, 1), :]
                first = pl.multiple_of(b * alpha_rows, alpha_rows)
                for j in range(states):
                    source = jnp.broadcast_to(turned_ref[j, pl.ds(b, 1), :], (8, LANES))
                    from_alpha = jnp.concatenate(
                        [
                            jnp.take_along_axis(source, aidx_ref[r : r + 8, :], axis=1)
                            for r in range(0, alpha_rows, 8)
                        ],
                        axis=0,
                    )
                    from_beta = picked[
                        j * alpha_rows : (j + 1) * alpha_rows, v * LANES : (v + 1) * LANES
                    ]
                    for half, asg, bsg in ((0, asf_ref, sf), (1, asb_ref, sb)):
                        value = asg[...] * from_alpha + bsg * from_beta
                        top, rest = split_two(value)
                        col = j * pairs + half * LANES
                        right_ref[pl.ds(first, alpha_rows), col : col + LANES] = top
                        low_ref[pl.ds(first, alpha_rows), col : col + LANES] = rest
        return carry

    lax.fori_loop(0, beta_rows // step, build, 0)

    depth = alpha_rows * beta_rows
    piece = 1024

    def turn(k, carry):
        first = pl.multiple_of(k * piece, piece)
        for ja in range(states):
            col = pl.multiple_of((my_alpha ^ ja) * pairs, pairs)
            value = lax.dot_general(
                perm_ref[...],
                right_ref[pl.ds(first, piece), pl.ds(col, pairs)],
                (((1,), (1,)), ((), ())),
                preferred_element_type=F32,
            )
            left_ref[ja * pairs : (ja + 1) * pairs, pl.ds(first, piece)] = value.astype(BF16)
        return carry

    lax.fori_loop(0, depth // piece, turn, 0)

    beta_bits = (pairs // rows_each).bit_length() - 1
    for ja in range(states):
        value = jnp.dot(
            left_ref[ja * pairs : (ja + 1) * pairs, :],
            right_ref[...],
            preferred_element_type=F32,
        )
        for jb in range(1 << beta_bits):
            rows = value[jb * rows_each : (jb + 1) * rows_each]
            first_col = 0
            for s in range(streams):
                place = 0
                for kind, bit in orders[s]:
                    source = jb if kind == "beta" else ja
                    place = 2 * place + ((source >> bit) & 1)
                target = send_refs[s] if jb & 1 else keep_refs[s]
                first_row = place * rows_each + (ONE_ROWS if s == streams - 1 else 0)
                target[first_row : first_row + rows_each, :] = rows[
                    :, first_col : first_col + columns[s]
                ]
                first_col += columns[s]

    one = jnp.dot(state_ref[...], right_ref[...], preferred_element_type=F32)
    one_low = jnp.dot(state_ref[...], low_ref[...], preferred_element_type=F32)
    total = one + one_low
    one = total[0:states] + total[states : 2 * states]
    one_rows = jnp.concatenate(
        [one[:, j * pairs : (j + 1) * pairs] for j in range(states)], axis=0
    )
    send_refs[-1][0:ONE_ROWS, :] = one_rows
    keep_refs[-1][0:ONE_ROWS, :] = one_rows


def last_kernel(groups, lane_ref, *refs):
    count = len(groups)
    kept, got = refs[:count], refs[count : 2 * count]
    one_ref, two_ref = refs[2 * count :]
    pairs = 2 * LANES
    back0, back1 = lane_ref[0:1, 0:LANES], lane_ref[0:1, LANES:pairs]
    sums = [kept[s][...] + got[s][...] for s in range(count)]
    one_rows = sums[-1][0:ONE_ROWS]
    states = ONE_ROWS // one_ref.shape[0]
    sums[-1] = sums[-1][ONE_ROWS:]
    value = jnp.concatenate(sums, axis=1)

    def place(whole, out_ref, first_col):
        rows, total = whole.shape
        for col in range(0, total, pairs):
            for r in range(0, rows, 8):
                n = min(8, rows - r)
                left = whole[r : r + n, col : col + LANES]
                right = whole[r : r + n, col + LANES : col + pairs]
                if n < 8:
                    left = jnp.concatenate([left] * (8 // n), axis=0)
                    right = jnp.concatenate([right] * (8 // n), axis=0)
                to = first_col + col
                out_ref[r : r + n, to : to + LANES] = pick_lanes(left, right, back0)[0:n]
                out_ref[r : r + n, to + LANES : to + pairs] = pick_lanes(left, right, back1)[0:n]

    place(value, two_ref, 0)
    rows = one_ref.shape[0]
    for j in range(states):
        place(one_rows[j * rows : (j + 1) * rows], one_ref, j * pairs)


def swap(value, kind, flip, sizes):
    return lax.ppermute(value, kind, [(i, i ^ flip) for i in range(sizes[kind])])


def shards(sizes, ci_vectors, alpha_source, alpha_sign, beta_source, beta_sign):
    states, alpha_rows, beta_rows = ci_vectors.shape
    pairs = alpha_source.shape[1]
    total = states * pairs
    norb = int(round(pairs ** 0.5))
    forward, backward = pair_lanes(norb)
    lane = np.concatenate([forward, backward]).reshape(1, pairs)
    inverse = np.argsort(lane[0]).astype(np.int32).reshape(1, pairs)
    rows_each = total // (sizes["alpha"] * sizes["beta"])
    alpha_bits = sizes["alpha"].bit_length() - 1
    beta_bits = sizes["beta"].bit_length() - 1

    beta_parts = [ci_vectors] + [None] * (sizes["beta"] - 1)
    alpha_parts = [ci_vectors] + [None] * (sizes["alpha"] - 1)
    beta_parts[1] = swap(ci_vectors, "beta", 1, sizes)
    for j in range(2, sizes["beta"], 2):
        beta_parts[j] = swap(ci_vectors, "beta", j, sizes)
    for j in range(2, sizes["alpha"], 2):
        alpha_parts[j] = swap(ci_vectors, "alpha", j, sizes)
    for j in range(0, sizes["alpha"], 2):
        alpha_parts[j + 1] = swap(alpha_parts[j], "alpha", 1, sizes)
    for j in range(2, sizes["beta"], 2):
        beta_parts[j + 1] = swap(beta_parts[j], "beta", 1, sizes)
    late, _ = lax.optimization_barrier((ci_vectors, (alpha_parts[2], beta_parts[-2])))
    flat = jnp.transpose(late, (0, 2, 1)).reshape(states, alpha_rows * beta_rows)

    in_beta = [("beta", i) for i in range(1, beta_bits)]
    in_alpha = [("alpha", i) for i in range(alpha_bits)]
    orders = [
        in_beta + in_alpha,
        in_beta[::-1] + in_alpha,
        in_alpha + in_beta,
    ]
    columns = [384, 384, 256]
    streams = len(orders)
    extra = [0, 0, ONE_ROWS]
    half = total // 2
    beta_count = sizes["beta"] * beta_rows
    depth = alpha_rows * beta_rows
    vmem = pl.BlockSpec(memory_space=pltpu.VMEM)
    results = pl.pallas_call(
        functools.partial(
            main_kernel, rows_each, orders, columns, (sizes["alpha"], sizes["beta"])
        ),
        out_shape=[
            jax.ShapeDtypeStruct((half + extra[s], columns[s]), F32) for s in range(streams)
        ]
        * 2,
        in_specs=[vmem] * 6
        + [pl.BlockSpec(memory_space=pltpu.HBM)] * (sizes["alpha"] + sizes["beta"] - 1),
        out_specs=[vmem] * (2 * streams),
        scratch_shapes=[
            pltpu.VMEM((2 * states * alpha_rows, beta_count), BF16),
            pltpu.VMEM((states, beta_rows, sizes["alpha"] * alpha_rows), F32),
            pltpu.VMEM((alpha_rows, LANES), jnp.int32),
            pltpu.VMEM((alpha_rows, LANES), F32),
            pltpu.VMEM((alpha_rows, LANES), F32),
            pltpu.VMEM((beta_rows, LANES), jnp.int32),
            pltpu.VMEM((beta_rows, LANES), F32),
            pltpu.VMEM((beta_rows, LANES), F32),
            pltpu.VMEM((depth, total), BF16),
            pltpu.VMEM((depth, total), BF16),
            pltpu.VMEM((total, depth), BF16),
            pltpu.VMEM((16, depth), BF16),
            pltpu.VMEM((pairs, pairs), BF16),
            pltpu.VMEM((sizes["alpha"] + sizes["beta"] - 1,) + ci_vectors.shape, F32),
            pltpu.SemaphoreType.DMA((sizes["alpha"] + sizes["beta"] - 1,)),
        ],
        compiler_params=pltpu.CompilerParams(vmem_limit_bytes=58 << 20),
        name="excite",
    )(
        jnp.asarray(lane),
        flat,
        alpha_source,
        alpha_sign,
        beta_source,
        beta_sign,
        *alpha_parts,
        *beta_parts[1:],
    )
    send, keep = list(results[:streams]), list(results[streams:])
    got = [swap(send[s], "beta", 1, sizes) for s in range(streams)]
    for t in range(len(orders[0])):
        if t:
            keep, got = lax.optimization_barrier((keep, got))
        if len(keep) == 3 and orders[0][t:] == orders[1][t:]:
            keep = [jnp.concatenate(keep[:2], axis=1), keep[2]]
            got = [jnp.concatenate(got[:2], axis=1), got[2]]
            orders = orders[1:]
            extra = extra[1:]
        out = [None] * len(keep)
        for s in range(len(keep)):
            if s:
                out[s - 1], keep[s], got[s] = lax.optimization_barrier(
                    (out[s - 1], keep[s], got[s])
                )
            n = (keep[s].shape[0] - extra[s]) // 2 + extra[s]
            out[s] = keep[s][n:] + got[s][n:]
            if extra[s]:
                out[s] = jnp.concatenate([keep[s][: extra[s]] + got[s][: extra[s]], out[s]], axis=0)
            keep[s] = keep[s][:n] + got[s][:n]
        for s in range(len(keep)):
            kind, bit = orders[s][t]
            got[s] = swap(out[s], kind, 1 << bit, sizes)
    one_body, two_body = pl.pallas_call(
        functools.partial(last_kernel, [k.shape[1] for k in keep]),
        out_shape=[
            jax.ShapeDtypeStruct((states, total), F32),
            jax.ShapeDtypeStruct((rows_each, total), F32),
        ],
        in_specs=[vmem] * (1 + 2 * len(keep)),
        out_specs=[vmem] * 2,
        name="finish",
    )(jnp.asarray(inverse), *keep, *got)
    return (one_body, two_body)


def solution(mesh):
    return jax.shard_map(
        functools.partial(shards, dict(mesh.shape)),
        mesh=mesh,
        in_specs=(
            P(None, "alpha", "beta"),
            P("alpha", None),
            P("alpha", None),
            P("beta", None),
            P("beta", None),
        ),
        out_specs=(P(), P(("alpha", "beta"), None)),
        check_vma=False,
    )
```

```python
import functools

import jax
import jax.numpy as jnp
import numpy as np
from jax import lax
from jax.experimental import pallas as pl
from jax.experimental.pallas import tpu as pltpu
from jax.sharding import PartitionSpec as P

F32 = jnp.float32
BF16 = jnp.bfloat16
LANES = 128
ONE_ROWS = 16


def pair_lanes(norb):
    forward, backward = [], []
    for p in range(norb):
        for q in range(p + 1, norb):
            forward.append(p * norb + q)
            backward.append(q * norb + p)
    for p in range(norb // 2):
        forward.append(p * (norb + 1))
        backward.append((p + norb // 2) * (norb + 1))
    return np.array(forward, np.int32), np.array(backward, np.int32)


def pick_lanes(left, right, lane):
    low = jnp.broadcast_to(lane & (LANES - 1), left.shape)
    from_left = jnp.take_along_axis(left, low, axis=1)
    from_right = jnp.take_along_axis(right, low, axis=1)
    return jnp.where(lane < LANES, from_left, from_right)


def split_two(value):
    high = value.astype(BF16)
    return high, (value - high.astype(F32)).astype(BF16)


def main_kernel(
    rows_each,
    orders,
    columns,
    parts,
    lane_ref,
    asrc_ref,
    asgn_ref,
    bsrc_ref,
    bsgn_ref,
    *refs,
):
    alpha_parts, beta_parts = parts
    count = alpha_parts + beta_parts - 1
    given, refs = refs[:count], refs[count:]
    parts_ref, sems = refs[-2:]
    copies = [
        pltpu.make_async_copy(given[k], parts_ref.at[k], sems.at[k]) for k in range(count)
    ]
    for copy in copies:
        copy.start()
    streams = len(columns)
    send_refs = refs[:streams]
    keep_refs = refs[streams : 2 * streams]
    (
        table_ref,
        turned_ref,
        aidx_ref,
        asf_ref,
        asb_ref,
        bidx_ref,
        bsf_ref,
        bsb_ref,
        right_ref,
        low_ref,
        left_ref,
        state_ref,
        perm_ref,
        flat_ref,
    ) = refs[2 * streams : -2]
    states, alpha_rows, beta_rows = given[0].shape
    beta_count = beta_parts * beta_rows
    both = states * alpha_rows
    pairs = 2 * LANES
    my_alpha = lax.axis_index("alpha")
    my_beta = lax.axis_index("beta")
    forward = lane_ref[0:1, 0:LANES]
    backward = lane_ref[0:1, LANES:pairs]

    def tables(src_ref, sgn_ref, idx_ref, sf_ref, sb_ref, count, flip):
        for r in range(0, count, 8):
            rows = slice(r, r + 8)
            s0, s1 = sgn_ref[rows, 0:LANES], sgn_ref[rows, LANES:pairs]
            i0, i1 = src_ref[rows, 0:LANES], src_ref[rows, LANES:pairs]
            sf = pick_lanes(s0, s1, forward)
            sb = pick_lanes(s0, s1, backward)
            source = jnp.where(
                sf != 0, pick_lanes(i0, i1, forward), pick_lanes(i0, i1, backward)
            )
            idx_ref[rows, :] = source ^ flip
            sf_ref[rows, :] = sf.astype(F32)
            sb_ref[rows, :] = sb.astype(F32)

    tables(asrc_ref, asgn_ref, aidx_ref, asf_ref, asb_ref, alpha_rows, my_alpha * alpha_rows)
    tables(bsrc_ref, bsgn_ref, bidx_ref, bsf_ref, bsb_ref, beta_rows, my_beta * beta_rows)

    natural = lane_ref[0:1, :]
    row = lax.broadcasted_iota(jnp.int32, (pairs, pairs), 0)
    shift = rows_each.bit_length() - 1
    wanted = (((row >> shift) ^ my_beta) << shift) | (row & (rows_each - 1))
    perm_ref[...] = jnp.where(natural == wanted, 1.0, 0.0).astype(BF16)

    for copy in copies:
        copy.wait()
    for k in range(beta_parts):
        at = alpha_parts + k - 1 if k else 0
        high, mid = split_two(parts_ref[at].reshape(both, beta_rows))
        table_ref[0:both, k * beta_rows : (k + 1) * beta_rows] = high
        table_ref[both : 2 * both, k * beta_rows : (k + 1) * beta_rows] = mid
    for j in range(states):
        rows = jnp.concatenate([parts_ref[k, j] for k in range(alpha_parts)], axis=0)
        turned_ref[j] = rows.T

    per = LANES // alpha_rows
    groups = beta_rows // per
    for j in range(states):
        lines = jnp.concatenate(
            [turned_ref[j, pl.ds(q, groups, stride=per), 0:alpha_rows] for q in range(per)],
            axis=1,
        )
        for g in range(groups):
            flat_ref[j : j + 1, g * LANES : (g + 1) * LANES] = lines[g : g + 1, :]
    flat = flat_ref[...]
    flat_high = flat.astype(BF16).astype(F32)
    pad = jnp.zeros((16 - 2 * states, flat.shape[1]), F32)
    state_ref[...] = jnp.concatenate([flat_high, flat - flat_high, pad], axis=0).astype(BF16)

    chunk = min(1024, beta_count)
    chunks = beta_count // chunk
    step = 16

    def one_hot_dot(idx0, idx1, first):
        where = lax.broadcasted_iota(jnp.int32, (chunk, LANES), 0) + first
        picks = jnp.concatenate(
            [
                jnp.where(where == idx0, 1.0, 0.0).astype(BF16),
                jnp.where(where == idx1, 1.0, 0.0).astype(BF16),
            ],
            axis=1,
        )
        if chunks == 1:
            part = table_ref[...]
        else:
            part = table_ref[:, pl.ds(pl.multiple_of(first, chunk), chunk)]
        return jnp.dot(part, picks, preferred_element_type=F32)

    def build(block, carry):
        for u in range(step // 2):
            b0 = block * step + 2 * u
            idx0 = bidx_ref[pl.ds(b0, 1), :]
            idx1 = bidx_ref[pl.ds(b0 + 1, 1), :]
            if chunks == 1:
                got = one_hot_dot(idx0, idx1, 0)
            else:
                got = lax.fori_loop(
                    0,
                    chunks,
                    lambda c, acc: acc + one_hot_dot(idx0, idx1, c * chunk),
                    jnp.zeros((2 * both, 2 * LANES), F32),
                )
            picked = got[0:both] + got[both : 2 * both]
            for v in range(2):
                b = b0 + v
                sf = bsf_ref[pl.ds(b, 1), :]
                sb = bsb_ref[pl.ds(b, 1), :]
                first = pl.multiple_of(b * alpha_rows, alpha_rows)
                for j in range(states):
                    source = jnp.broadcast_to(turned_ref[j, pl.ds(b, 1), :], (8, LANES))
                    from_alpha = jnp.concatenate(
                        [
                            jnp.take_along_axis(source, aidx_ref[r : r + 8, :], axis=1)
                            for r in range(0, alpha_rows, 8)
                        ],
                        axis=0,
                    )
                    from_beta = picked[
                        j * alpha_rows : (j + 1) * alpha_rows, v * LANES : (v + 1) * LANES
                    ]
                    for half, asg, bsg in ((0, asf_ref, sf), (1, asb_ref, sb)):
                        value = asg[...] * from_alpha + bsg * from_beta
                        top, rest = split_two(value)
                        col = j * pairs + half * LANES
                        right_ref[pl.ds(first, alpha_rows), col : col + LANES] = top
                        low_ref[pl.ds(first, alpha_rows), col : col + LANES] = rest
        return carry

    lax.fori_loop(0, beta_rows // step, build, 0)

    depth = alpha_rows * beta_rows
    piece = 1024

    def turn(k, carry):
        first = pl.multiple_of(k * piece, piece)
        for ja in range(states):
            col = pl.multiple_of((my_alpha ^ ja) * pairs, pairs)
            value = lax.dot_general(
                perm_ref[...],
                right_ref[pl.ds(first, piece), pl.ds(col, pairs)],
                (((1,), (1,)), ((), ())),
                preferred_element_type=F32,
            )
            left_ref[ja * pairs : (ja + 1) * pairs, pl.ds(first, piece)] = value.astype(BF16)
        return carry

    lax.fori_loop(0, depth // piece, turn, 0)

    beta_bits = (pairs // rows_each).bit_length() - 1
    for ja in range(states):
        value = jnp.dot(
            left_ref[ja * pairs : (ja + 1) * pairs, :],
            right_ref[...],
            preferred_element_type=F32,
        )
        for jb in range(1 << beta_bits):
            rows = value[jb * rows_each : (jb + 1) * rows_each]
            first_col = 0
            for s in range(streams):
                place = 0
                for kind, bit in orders[s]:
                    source = jb if kind == "beta" else ja
                    place = 2 * place + ((source >> bit) & 1)
                target = send_refs[s] if jb & 1 else keep_refs[s]
                first_row = place * rows_each + (ONE_ROWS if s == streams - 1 else 0)
                target[first_row : first_row + rows_each, :] = rows[
                    :, first_col : first_col + columns[s]
                ]
                first_col += columns[s]

    one = jnp.dot(state_ref[...], right_ref[...], preferred_element_type=F32)
    one_low = jnp.dot(state_ref[...], low_ref[...], preferred_element_type=F32)
    total = one + one_low
    one = total[0:states] + total[states : 2 * states]
    one_rows = jnp.concatenate(
        [one[:, j * pairs : (j + 1) * pairs] for j in range(states)], axis=0
    )
    send_refs[-1][0:ONE_ROWS, :] = one_rows
    keep_refs[-1][0:ONE_ROWS, :] = one_rows


def last_kernel(groups, lane_ref, *refs):
    count = len(groups)
    kept, got = refs[:count], refs[count : 2 * count]
    one_ref, two_ref = refs[2 * count :]
    pairs = 2 * LANES
    back0, back1 = lane_ref[0:1, 0:LANES], lane_ref[0:1, LANES:pairs]
    sums = [kept[s][...] + got[s][...] for s in range(count)]
    one_rows = sums[-1][0:ONE_ROWS]
    states = ONE_ROWS // one_ref.shape[0]
    sums[-1] = sums[-1][ONE_ROWS:]
    value = jnp.concatenate(sums, axis=1)

    def place(whole, out_ref, first_col):
        rows, total = whole.shape
        for col in range(0, total, pairs):
            for r in range(0, rows, 8):
                n = min(8, rows - r)
                left = whole[r : r + n, col : col + LANES]
                right = whole[r : r + n, col + LANES : col + pairs]
                if n < 8:
                    left = jnp.concatenate([left] * (8 // n), axis=0)
                    right = jnp.concatenate([right] * (8 // n), axis=0)
                to = first_col + col
                out_ref[r : r + n, to : to + LANES] = pick_lanes(left, right, back0)[0:n]
                out_ref[r : r + n, to + LANES : to + pairs] = pick_lanes(left, right, back1)[0:n]

    place(value, two_ref, 0)
    rows = one_ref.shape[0]
    for j in range(states):
        place(one_rows[j * rows : (j + 1) * rows], one_ref, j * pairs)


def swap(value, kind, flip, sizes):
    return lax.ppermute(value, kind, [(i, i ^ flip) for i in range(sizes[kind])])


def shards(sizes, ci_vectors, alpha_source, alpha_sign, beta_source, beta_sign):
    states, alpha_rows, beta_rows = ci_vectors.shape
    pairs = alpha_source.shape[1]
    total = states * pairs
    norb = int(round(pairs ** 0.5))
    forward, backward = pair_lanes(norb)
    lane = np.concatenate([forward, backward]).reshape(1, pairs)
    inverse = np.argsort(lane[0]).astype(np.int32).reshape(1, pairs)
    rows_each = total // (sizes["alpha"] * sizes["beta"])
    alpha_bits = sizes["alpha"].bit_length() - 1
    beta_bits = sizes["beta"].bit_length() - 1

    beta_parts = [ci_vectors] + [None] * (sizes["beta"] - 1)
    alpha_parts = [ci_vectors] + [None] * (sizes["alpha"] - 1)
    beta_parts[1] = swap(ci_vectors, "beta", 1, sizes)
    for j in range(2, sizes["beta"], 2):
        beta_parts[j] = swap(ci_vectors, "beta", j, sizes)
    for j in range(1, sizes["alpha"]):
        alpha_parts[j] = swap(ci_vectors, "alpha", j, sizes)
    for j in range(2, sizes["beta"], 2):
        beta_parts[j + 1] = swap(beta_parts[j], "beta", 1, sizes)

    in_beta = [("beta", i) for i in range(1, beta_bits)]
    in_alpha = [("alpha", i) for i in range(alpha_bits)]
    orders = [
        in_beta + in_alpha,
        in_beta[::-1] + in_alpha,
        in_alpha + in_beta,
    ]
    columns = [384, 384, 256]
    streams = len(orders)
    extra = [0, 0, ONE_ROWS]
    half = total // 2
    beta_count = sizes["beta"] * beta_rows
    depth = alpha_rows * beta_rows
    vmem = pl.BlockSpec(memory_space=pltpu.VMEM)
    results = pl.pallas_call(
        functools.partial(
            main_kernel, rows_each, orders, columns, (sizes["alpha"], sizes["beta"])
        ),
        out_shape=[
            jax.ShapeDtypeStruct((half + extra[s], columns[s]), F32) for s in range(streams)
        ]
        * 2,
        in_specs=[vmem] * 5
        + [pl.BlockSpec(memory_space=pltpu.HBM)] * (sizes["alpha"] + sizes["beta"] - 1),
        out_specs=[vmem] * (2 * streams),
        scratch_shapes=[
            pltpu.VMEM((2 * states * alpha_rows, beta_count), BF16),
            pltpu.VMEM((states, beta_rows, sizes["alpha"] * alpha_rows), F32),
            pltpu.VMEM((alpha_rows, LANES), jnp.int32),
            pltpu.VMEM((alpha_rows, LANES), F32),
            pltpu.VMEM((alpha_rows, LANES), F32),
            pltpu.VMEM((beta_rows, LANES), jnp.int32),
            pltpu.VMEM((beta_rows, LANES), F32),
            pltpu.VMEM((beta_rows, LANES), F32),
            pltpu.VMEM((depth, total), BF16),
            pltpu.VMEM((depth, total), BF16),
            pltpu.VMEM((total, depth), BF16),
            pltpu.VMEM((16, depth), BF16),
            pltpu.VMEM((pairs, pairs), BF16),
            pltpu.VMEM((states, depth), F32),
            pltpu.VMEM((sizes["alpha"] + sizes["beta"] - 1,) + ci_vectors.shape, F32),
            pltpu.SemaphoreType.DMA((sizes["alpha"] + sizes["beta"] - 1,)),
        ],
        compiler_params=pltpu.CompilerParams(vmem_limit_bytes=58 << 20),
        name="excite",
    )(
        jnp.asarray(lane),
        alpha_source,
        alpha_sign,
        beta_source,
        beta_sign,
        *alpha_parts,
        *beta_parts[1:],
    )
    send, keep = list(results[:streams]), list(results[streams:])
    got = [swap(send[s], "beta", 1, sizes) for s in range(streams)]
    for t in range(len(orders[0])):
        if 0 < t < 3:
            keep, got = lax.optimization_barrier((keep, got))
        if len(keep) == 3 and orders[0][t:] == orders[1][t:]:
            keep = [jnp.concatenate(keep[:2], axis=1), keep[2]]
            got = [jnp.concatenate(got[:2], axis=1), got[2]]
            orders = orders[1:]
            extra = extra[1:]
        out = [None] * len(keep)
        for s in range(len(keep)):
            if s and len(keep) == 3:
                out[s - 1], keep[s], got[s] = lax.optimization_barrier(
                    (out[s - 1], keep[s], got[s])
                )
            n = (keep[s].shape[0] - extra[s]) // 2 + extra[s]
            out[s] = keep[s][n:] + got[s][n:]
            if extra[s]:
                out[s] = jnp.concatenate([keep[s][: extra[s]] + got[s][: extra[s]], out[s]], axis=0)
            keep[s] = keep[s][:n] + got[s][:n]
        for s in range(len(keep)):
            kind, bit = orders[s][t]
            got[s] = swap(out[s], kind, 1 << bit, sizes)
    one_body, two_body = pl.pallas_call(
        functools.partial(last_kernel, [k.shape[1] for k in keep]),
        out_shape=[
            jax.ShapeDtypeStruct((states, total), F32),
            jax.ShapeDtypeStruct((rows_each, total), F32),
        ],
        in_specs=[vmem] * (1 + 2 * len(keep)),
        out_specs=[vmem] * 2,
        name="finish",
    )(jnp.asarray(inverse), *keep, *got)
    return (one_body, two_body)


def solution(mesh):
    return jax.shard_map(
        functools.partial(shards, dict(mesh.shape)),
        mesh=mesh,
        in_specs=(
            P(None, "alpha", "beta"),
            P("alpha", None),
            P("alpha", None),
            P("beta", None),
            P("beta", None),
        ),
        out_specs=(P(), P(("alpha", "beta"), None)),
        check_vma=False,
    )
```

```python
import functools

import jax
import jax.numpy as jnp
import numpy as np
from jax import lax
from jax.experimental import pallas as pl
from jax.experimental.pallas import tpu as pltpu
from jax.sharding import PartitionSpec as P

F32 = jnp.float32
BF16 = jnp.bfloat16
LANES = 128
ONE_ROWS = 16


def pair_lanes(norb):
    forward, backward = [], []
    for p in range(norb):
        for q in range(p + 1, norb):
            forward.append(p * norb + q)
            backward.append(q * norb + p)
    for p in range(norb // 2):
        forward.append(p * (norb + 1))
        backward.append((p + norb // 2) * (norb + 1))
    return np.array(forward, np.int32), np.array(backward, np.int32)


def pick_lanes(left, right, lane):
    low = jnp.broadcast_to(lane & (LANES - 1), left.shape)
    from_left = jnp.take_along_axis(left, low, axis=1)
    from_right = jnp.take_along_axis(right, low, axis=1)
    return jnp.where(lane < LANES, from_left, from_right)


def split_two(value):
    high = value.astype(BF16)
    return high, (value - high.astype(F32)).astype(BF16)


def main_kernel(
    rows_each,
    orders,
    columns,
    parts,
    lane_ref,
    asrc_ref,
    asgn_ref,
    bsrc_ref,
    bsgn_ref,
    *refs,
):
    alpha_parts, beta_parts = parts
    count = alpha_parts + beta_parts - 1
    given, refs = refs[:count], refs[count:]
    parts_ref, sems = refs[-2:]
    copies = [
        pltpu.make_async_copy(given[k], parts_ref.at[k], sems.at[k]) for k in range(count)
    ]
    for copy in copies:
        copy.start()
    streams = len(columns)
    send_refs = refs[:streams]
    keep_refs = refs[streams : 2 * streams]
    (
        table_ref,
        turned_ref,
        aidx_ref,
        asf_ref,
        asb_ref,
        bidx_ref,
        bsf_ref,
        bsb_ref,
        right_ref,
        low_ref,
        left_ref,
        state_ref,
        perm_ref,
        flat_ref,
    ) = refs[2 * streams : -2]
    states, alpha_rows, beta_rows = given[0].shape
    beta_count = beta_parts * beta_rows
    both = states * alpha_rows
    pairs = 2 * LANES
    my_alpha = lax.axis_index("alpha")
    my_beta = lax.axis_index("beta")
    forward = lane_ref[0:1, 0:LANES]
    backward = lane_ref[0:1, LANES:pairs]

    def tables(src_ref, sgn_ref, idx_ref, sf_ref, sb_ref, count, flip):
        for r in range(0, count, 8):
            rows = slice(r, r + 8)
            s0, s1 = sgn_ref[rows, 0:LANES], sgn_ref[rows, LANES:pairs]
            i0, i1 = src_ref[rows, 0:LANES], src_ref[rows, LANES:pairs]
            sf = pick_lanes(s0, s1, forward)
            sb = pick_lanes(s0, s1, backward)
            source = jnp.where(
                sf != 0, pick_lanes(i0, i1, forward), pick_lanes(i0, i1, backward)
            )
            idx_ref[rows, :] = source ^ flip
            sf_ref[rows, :] = sf.astype(F32)
            sb_ref[rows, :] = sb.astype(F32)

    tables(asrc_ref, asgn_ref, aidx_ref, asf_ref, asb_ref, alpha_rows, my_alpha * alpha_rows)
    tables(bsrc_ref, bsgn_ref, bidx_ref, bsf_ref, bsb_ref, beta_rows, my_beta * beta_rows)

    natural = lane_ref[0:1, :]
    row = lax.broadcasted_iota(jnp.int32, (pairs, pairs), 0)
    shift = rows_each.bit_length() - 1
    wanted = (((row >> shift) ^ my_beta) << shift) | (row & (rows_each - 1))
    perm_ref[...] = jnp.where(natural == wanted, 1.0, 0.0).astype(BF16)

    for copy in copies:
        copy.wait()
    for k in range(beta_parts):
        at = alpha_parts + k - 1 if k else 0
        high, mid = split_two(parts_ref[at].reshape(both, beta_rows))
        table_ref[0:both, k * beta_rows : (k + 1) * beta_rows] = high
        table_ref[both : 2 * both, k * beta_rows : (k + 1) * beta_rows] = mid
    for j in range(states):
        rows = jnp.concatenate([parts_ref[k, j] for k in range(alpha_parts)], axis=0)
        turned_ref[j] = rows.T

    per = LANES // alpha_rows
    groups = beta_rows // per
    for j in range(states):
        lines = jnp.concatenate(
            [turned_ref[j, pl.ds(q, groups, stride=per), 0:alpha_rows] for q in range(per)],
            axis=1,
        )
        for g in range(groups):
            flat_ref[j : j + 1, g * LANES : (g + 1) * LANES] = lines[g : g + 1, :]
    flat = flat_ref[...]
    flat_high = flat.astype(BF16).astype(F32)
    pad = jnp.zeros((16 - 2 * states, flat.shape[1]), F32)
    state_ref[...] = jnp.concatenate([flat_high, flat - flat_high, pad], axis=0).astype(BF16)

    chunk = min(1024, beta_count)
    chunks = beta_count // chunk
    step = 16

    def one_hot_dot(idx0, idx1, first):
        where = lax.broadcasted_iota(jnp.int32, (chunk, LANES), 0) + first
        picks = jnp.concatenate(
            [
                jnp.where(where == idx0, 1.0, 0.0).astype(BF16),
                jnp.where(where == idx1, 1.0, 0.0).astype(BF16),
            ],
            axis=1,
        )
        if chunks == 1:
            part = table_ref[...]
        else:
            part = table_ref[:, pl.ds(pl.multiple_of(first, chunk), chunk)]
        return jnp.dot(part, picks, preferred_element_type=F32)

    def build(block, carry):
        for u in range(step // 2):
            b0 = block * step + 2 * u
            idx0 = bidx_ref[pl.ds(b0, 1), :]
            idx1 = bidx_ref[pl.ds(b0 + 1, 1), :]
            if chunks == 1:
                got = one_hot_dot(idx0, idx1, 0)
            else:
                got = lax.fori_loop(
                    0,
                    chunks,
                    lambda c, acc: acc + one_hot_dot(idx0, idx1, c * chunk),
                    jnp.zeros((2 * both, 2 * LANES), F32),
                )
            picked = got[0:both] + got[both : 2 * both]
            for v in range(2):
                b = b0 + v
                sf = bsf_ref[pl.ds(b, 1), :]
                sb = bsb_ref[pl.ds(b, 1), :]
                first = pl.multiple_of(b * alpha_rows, alpha_rows)
                for j in range(states):
                    source = jnp.broadcast_to(turned_ref[j, pl.ds(b, 1), :], (8, LANES))
                    from_alpha = jnp.concatenate(
                        [
                            jnp.take_along_axis(source, aidx_ref[r : r + 8, :], axis=1)
                            for r in range(0, alpha_rows, 8)
                        ],
                        axis=0,
                    )
                    from_beta = picked[
                        j * alpha_rows : (j + 1) * alpha_rows, v * LANES : (v + 1) * LANES
                    ]
                    for half, asg, bsg in ((0, asf_ref, sf), (1, asb_ref, sb)):
                        value = asg[...] * from_alpha + bsg * from_beta
                        top, rest = split_two(value)
                        col = j * pairs + half * LANES
                        right_ref[pl.ds(first, alpha_rows), col : col + LANES] = top
                        low_ref[pl.ds(first, alpha_rows), col : col + LANES] = rest
        return carry

    lax.fori_loop(0, beta_rows // step, build, 0)

    depth = alpha_rows * beta_rows
    piece = 1024

    def turn(k, carry):
        first = pl.multiple_of(k * piece, piece)
        for ja in range(states):
            col = pl.multiple_of((my_alpha ^ ja) * pairs, pairs)
            value = lax.dot_general(
                perm_ref[...],
                right_ref[pl.ds(first, piece), pl.ds(col, pairs)],
                (((1,), (1,)), ((), ())),
                preferred_element_type=F32,
            )
            left_ref[ja * pairs : (ja + 1) * pairs, pl.ds(first, piece)] = value.astype(BF16)
        return carry

    lax.fori_loop(0, depth // piece, turn, 0)

    beta_bits = (pairs // rows_each).bit_length() - 1
    for ja in range(states):
        value = jnp.dot(
            left_ref[ja * pairs : (ja + 1) * pairs, :],
            right_ref[...],
            preferred_element_type=F32,
        )
        for jb in range(1 << beta_bits):
            rows = value[jb * rows_each : (jb + 1) * rows_each]
            first_col = 0
            for s in range(streams):
                place = 0
                for kind, bit in orders[s]:
                    source = jb if kind == "beta" else ja
                    place = 2 * place + ((source >> bit) & 1)
                target = send_refs[s] if jb & 1 else keep_refs[s]
                first_row = place * rows_each + (ONE_ROWS if s == streams - 1 else 0)
                target[first_row : first_row + rows_each, :] = rows[
                    :, first_col : first_col + columns[s]
                ]
                first_col += columns[s]

    one = jnp.dot(state_ref[...], right_ref[...], preferred_element_type=F32)
    one_low = jnp.dot(state_ref[...], low_ref[...], preferred_element_type=F32)
    total = one + one_low
    one = total[0:states] + total[states : 2 * states]
    one_rows = jnp.concatenate(
        [one[:, j * pairs : (j + 1) * pairs] for j in range(states)], axis=0
    )
    send_refs[-1][0:ONE_ROWS, :] = one_rows
    keep_refs[-1][0:ONE_ROWS, :] = one_rows


def last_kernel(groups, lane_ref, *refs):
    count = len(groups)
    kept, got = refs[:count], refs[count : 2 * count]
    one_ref, two_ref = refs[2 * count :]
    pairs = 2 * LANES
    back0, back1 = lane_ref[0:1, 0:LANES], lane_ref[0:1, LANES:pairs]
    sums = [kept[s][...] + got[s][...] for s in range(count)]
    one_rows = sums[-1][0:ONE_ROWS]
    states = ONE_ROWS // one_ref.shape[0]
    sums[-1] = sums[-1][ONE_ROWS:]
    value = jnp.concatenate(sums, axis=1)

    def place(whole, out_ref, first_col):
        rows, total = whole.shape
        for col in range(0, total, pairs):
            for r in range(0, rows, 8):
                n = min(8, rows - r)
                left = whole[r : r + n, col : col + LANES]
                right = whole[r : r + n, col + LANES : col + pairs]
                if n < 8:
                    left = jnp.concatenate([left] * (8 // n), axis=0)
                    right = jnp.concatenate([right] * (8 // n), axis=0)
                to = first_col + col
                out_ref[r : r + n, to : to + LANES] = pick_lanes(left, right, back0)[0:n]
                out_ref[r : r + n, to + LANES : to + pairs] = pick_lanes(left, right, back1)[0:n]

    place(value, two_ref, 0)
    rows = one_ref.shape[0]
    for j in range(states):
        place(one_rows[j * rows : (j + 1) * rows], one_ref, j * pairs)


def swap(value, kind, flip, sizes):
    return lax.ppermute(value, kind, [(i, i ^ flip) for i in range(sizes[kind])])


def shards(sizes, ci_vectors, alpha_source, alpha_sign, beta_source, beta_sign):
    states, alpha_rows, beta_rows = ci_vectors.shape
    pairs = alpha_source.shape[1]
    total = states * pairs
    norb = int(round(pairs ** 0.5))
    forward, backward = pair_lanes(norb)
    lane = np.concatenate([forward, backward]).reshape(1, pairs)
    inverse = np.argsort(lane[0]).astype(np.int32).reshape(1, pairs)
    rows_each = total // (sizes["alpha"] * sizes["beta"])
    alpha_bits = sizes["alpha"].bit_length() - 1
    beta_bits = sizes["beta"].bit_length() - 1

    beta_parts = [ci_vectors] + [None] * (sizes["beta"] - 1)
    alpha_parts = [ci_vectors] + [None] * (sizes["alpha"] - 1)
    beta_parts[1] = swap(ci_vectors, "beta", 1, sizes)
    for j in range(2, sizes["beta"], 2):
        beta_parts[j] = swap(ci_vectors, "beta", j, sizes)
    for j in range(1, sizes["alpha"]):
        alpha_parts[j] = swap(ci_vectors, "alpha", j, sizes)
    for j in range(2, sizes["beta"], 2):
        beta_parts[j + 1] = swap(beta_parts[j], "beta", 1, sizes)

    in_beta = [("beta", i) for i in range(1, beta_bits)]
    in_alpha = [("alpha", i) for i in range(alpha_bits)]
    orders = [
        in_beta + in_alpha,
        in_beta[::-1] + in_alpha,
        in_alpha + in_beta,
    ]
    columns = [384, 384, 256]
    streams = len(orders)
    extra = [0, 0, ONE_ROWS]
    half = total // 2
    beta_count = sizes["beta"] * beta_rows
    depth = alpha_rows * beta_rows
    vmem = pl.BlockSpec(memory_space=pltpu.VMEM)
    results = pl.pallas_call(
        functools.partial(
            main_kernel, rows_each, orders, columns, (sizes["alpha"], sizes["beta"])
        ),
        out_shape=[
            jax.ShapeDtypeStruct((half + extra[s], columns[s]), F32) for s in range(streams)
        ]
        * 2,
        in_specs=[vmem] * 5
        + [pl.BlockSpec(memory_space=pltpu.HBM)] * (sizes["alpha"] + sizes["beta"] - 1),
        out_specs=[vmem] * (2 * streams),
        scratch_shapes=[
            pltpu.VMEM((2 * states * alpha_rows, beta_count), BF16),
            pltpu.VMEM((states, beta_rows, sizes["alpha"] * alpha_rows), F32),
            pltpu.VMEM((alpha_rows, LANES), jnp.int32),
            pltpu.VMEM((alpha_rows, LANES), F32),
            pltpu.VMEM((alpha_rows, LANES), F32),
            pltpu.VMEM((beta_rows, LANES), jnp.int32),
            pltpu.VMEM((beta_rows, LANES), F32),
            pltpu.VMEM((beta_rows, LANES), F32),
            pltpu.VMEM((depth, total), BF16),
            pltpu.VMEM((depth, total), BF16),
            pltpu.VMEM((total, depth), BF16),
            pltpu.VMEM((16, depth), BF16),
            pltpu.VMEM((pairs, pairs), BF16),
            pltpu.VMEM((states, depth), F32),
            pltpu.VMEM((sizes["alpha"] + sizes["beta"] - 1,) + ci_vectors.shape, F32),
            pltpu.SemaphoreType.DMA((sizes["alpha"] + sizes["beta"] - 1,)),
        ],
        compiler_params=pltpu.CompilerParams(vmem_limit_bytes=58 << 20),
        name="excite",
    )(
        jnp.asarray(lane),
        alpha_source,
        alpha_sign,
        beta_source,
        beta_sign,
        *alpha_parts,
        *beta_parts[1:],
    )
    send, keep = list(results[:streams]), list(results[streams:])
    got = [swap(send[s], "beta", 1, sizes) for s in range(streams)]
    for t in range(len(orders[0])):
        if t == 1:
            keep, got = lax.optimization_barrier((keep, got))
        if len(keep) == 3 and orders[0][t:] == orders[1][t:]:
            keep = [jnp.concatenate(keep[:2], axis=1), keep[2]]
            got = [jnp.concatenate(got[:2], axis=1), got[2]]
            orders = orders[1:]
            extra = extra[1:]
        out = [None] * len(keep)
        for s in range(len(keep)):
            if s and len(keep) == 3:
                out[s - 1], keep[s], got[s] = lax.optimization_barrier(
                    (out[s - 1], keep[s], got[s])
                )
            n = (keep[s].shape[0] - extra[s]) // 2 + extra[s]
            out[s] = keep[s][n:] + got[s][n:]
            if extra[s]:
                out[s] = jnp.concatenate([keep[s][: extra[s]] + got[s][: extra[s]], out[s]], axis=0)
            keep[s] = keep[s][:n] + got[s][:n]
        for s in range(len(keep)):
            kind, bit = orders[s][t]
            got[s] = swap(out[s], kind, 1 << bit, sizes)
    one_body, two_body = pl.pallas_call(
        functools.partial(last_kernel, [k.shape[1] for k in keep]),
        out_shape=[
            jax.ShapeDtypeStruct((states, total), F32),
            jax.ShapeDtypeStruct((rows_each, total), F32),
        ],
        in_specs=[vmem] * (1 + 2 * len(keep)),
        out_specs=[vmem] * 2,
        name="finish",
    )(jnp.asarray(inverse), *keep, *got)
    return (one_body, two_body)


def solution(mesh):
    return jax.shard_map(
        functools.partial(shards, dict(mesh.shape)),
        mesh=mesh,
        in_specs=(
            P(None, "alpha", "beta"),
            P("alpha", None),
            P("alpha", None),
            P("beta", None),
            P("beta", None),
        ),
        out_specs=(P(), P(("alpha", "beta"), None)),
        check_vma=False,
    )
```
